32 devices in a mesh: frame: 8 (over z, y), row: 4 (over x, core).
Axes of the slice: x: 2, y: 2, z: 4, core: 2. Of those that a mesh axis runs over, the one named last changes fastest.
Arguments:
- frames_x: bfloat16 [8, 24, 128, 512], P('frame', 'row'), may hold values from -6 to 6
- conv_weight: bfloat16 [3, 3, 512, 512], replicated, may hold values from -0.09375 to 0.09375
- conv_bias: float32 [512], replicated, may hold values from -3 to 3
- query_weight: bfloat16 [512, 512], replicated, may hold values from -0.25 to 0.25
- key_weight: bfloat16 [512, 512], replicated, may hold values from -0.25 to 0.25
- value_weight: bfloat16 [512, 512], replicated, may hold values from -0.25 to 0.25
- out_weight: bfloat16 [512, 512], replicated, may hold values from -0.25 to 0.25
- query_gain: float32 [512], replicated, may hold values from 0.5 to 2
- key_gain: float32 [512], replicated, may hold values from 0.5 to 2
- source_ids: int32 [8, 24, 4], P('frame', 'row'), may hold values from 0 to 23, as said below
- valid_counts: int32 [8, 24], P('frame', 'row'), may hold values from 1 to 4
Outputs:
- propagated: bfloat16 [8, 24, 128, 512], P('frame', 'row')
The draws below stay inside these ranges and needn't reach their ends.
Inputs may be any that keep to these rules, and one draw needn't show every extreme that they name: `source_ids`: block id s names row s // 1 of the previous frame, which lies at most 2 rows from the querying block's row; in every frame slot 0 of the blocks in even rows names a block 2 rows above and in odd rows 2 rows below, as far as the frame has that row.
All inputs are finite; a program needn't handle non-finite values.
Results may differ from the reference program's by a relative error of at most 0.0054.
Values may be sent and summed in bfloat16 or wider, within the bound.
A program may use at most 64 MiB of HBM per device.

```python
import math
import jax
import jax.numpy as jnp
from jax import lax

HEADS = 8
HD = 64
C = 512
KSRC = 4
BLOCK = 128
DISP = 2
W = 128
FRAMES = 8
H = 24
BPR = 1
NB = 24


def draw_source_ids(key, part):
    first_key, second_key = jax.random.split(jax.random.fold_in(key, 11))
    block_rows = jnp.arange(NB, dtype=jnp.int32) // BPR
    offsets = jax.random.randint(first_key, (FRAMES, NB, KSRC - 1), -DISP, DISP + 1)
    leading = jnp.where(block_rows % 2 == 0, -DISP, DISP).astype(jnp.int32)
    leading = jnp.broadcast_to(leading[None, :, None], (FRAMES, NB, 1))
    offsets = jnp.concatenate([leading, offsets.astype(jnp.int32)], axis=2)
    source_rows = jnp.clip(block_rows[None, :, None] + offsets, 0, H - 1)
    columns = jax.random.randint(second_key, (FRAMES, NB, KSRC), 0, BPR)
    return (source_rows * BPR + columns).astype(jnp.int32)


def plant(drawn, own_key, low, high):
    longest = drawn.shape.index(max(drawn.shape))
    spots = []
    for shift in (0, 1):
        where = [jax.random.randint(jax.random.fold_in(own_key, axis), (), 0, length) for axis, length in enumerate(drawn.shape)]
        where[longest] = (where[longest] + shift) % drawn.shape[longest]
        spots.append(tuple(where))
    return drawn.at[spots[0]].set(low).at[spots[1]].set(high)


def block_scale(stream_key, shape, shards, smallest, high):
    def one(position, blocks):
        draws = jax.random.uniform(jax.random.fold_in(jax.random.fold_in(stream_key, 6), position), (blocks,), jnp.float32, smallest / len(shards), high / len(shards))
        return jnp.repeat(jnp.exp(draws), shape[position] // blocks).reshape((-1,) + (1,) * (len(shape) - position - 1))

    factor_of = one(*shards[0])
    for cut in shards[1:]:
        factor_of = factor_of * one(*cut)
    return factor_of


def centred(own_key, extent, deviation, most, pieces=(), kind=jnp.bfloat16):
    array = deviation * jax.random.normal(own_key, extent, jnp.float32)
    if pieces:
        array = array * block_scale(own_key, extent, pieces, -0.22, 0.18)
    return jnp.clip(array, -most, most).astype(kind)


def setup_inputs(seed: int = 0) -> dict:
    streams_of = jax.random.split(jax.random.key(seed), 12)
    return {
        "frames_x": centred(streams_of[0], (FRAMES, H, W, C), 1.0, 6.0, ((0, 8), (1, 4))),
        "conv_weight": centred(streams_of[1], (3, 3, C, C), (9 * C) ** -0.5, 0.09375),
        "conv_bias": centred(streams_of[2], (C,), 0.5, 3.0, (), jnp.float32),
        "query_weight": centred(streams_of[3], (C, C), C ** -0.5, 0.25),
        "key_weight": centred(streams_of[4], (C, C), C ** -0.5, 0.25),
        "value_weight": centred(streams_of[5], (C, C), C ** -0.5, 0.25),
        "out_weight": centred(streams_of[6], (C, C), C ** -0.5, 0.25),
        "query_gain": jnp.clip(jnp.exp(jax.random.uniform(streams_of[7], (C,), jnp.float32, math.log(0.5), math.log(2.0))), 0.5, 2.0),
        "key_gain": jnp.clip(jnp.exp(jax.random.uniform(streams_of[8], (C,), jnp.float32, math.log(0.5), math.log(2.0))), 0.5, 2.0),
        "source_ids": draw_source_ids(jax.random.fold_in(streams_of[11], 71), 0),
        "valid_counts": plant(jax.random.randint(streams_of[10], (FRAMES, NB), 1, 5), jax.random.fold_in(streams_of[10], 1), 1, 4).astype(jnp.int32),
    }


def conv_frame(frame_in, conv_weight, conv_bias):
    padded = jnp.pad(frame_in, ((1, 1), (1, 1), (0, 0)))
    total = jnp.zeros((H * W, C), jnp.float32)
    for row_off in range(3):
        for col_off in range(3):
            window = padded[row_off:row_off + H, col_off:col_off + W].reshape(H * W, C)
            total = total + jnp.dot(window, conv_weight[row_off, col_off], preferred_element_type=jnp.float32)
    return (total + conv_bias).astype(jnp.bfloat16)

def normed(feats, weight, gain):
    proj = jnp.dot(feats, weight, preferred_element_type=jnp.float32).reshape(-1, HEADS, HD)
    proj = proj * lax.rsqrt(lax.optimization_barrier(jnp.mean(proj * proj, axis=-1, keepdims=True)) + 1e-06) * gain.reshape(HEADS, HD)
    return proj.reshape(-1, C).astype(jnp.bfloat16)

def attend(queries, key_set, value_set, mask):
    count = queries.shape[0]
    query_heads = queries.reshape(count, BLOCK, HEADS, HD).astype(jnp.float32)
    key_heads = key_set.reshape(count, -1, HEADS, HD).astype(jnp.float32)
    value_heads = value_set.reshape(count, -1, HEADS, HD).astype(jnp.float32)
    scores = jnp.einsum('nqhd,nkhd->nhqk', query_heads, key_heads) * HD ** (-0.5)
    expo = jnp.where(mask[:, None, None, :], jnp.exp(scores), 0.0)
    probs = (expo / lax.optimization_barrier(jnp.sum(expo, axis=-1, keepdims=True))).astype(jnp.bfloat16)
    mixed = jnp.einsum('nhqk,nkhd->nqhd', probs.astype(jnp.float32), value_heads)
    return mixed.reshape(count * BLOCK, C).astype(jnp.bfloat16)

def reference(frames_x, conv_weight, conv_bias, query_weight, key_weight, value_weight, out_weight, query_gain, key_gain, source_ids, valid_counts):
    feats_all = lax.map(lambda one: conv_frame(one, conv_weight, conv_bias), frames_x)
    queries_all = lax.map(lambda one: normed(one, query_weight, query_gain), feats_all)
    keys_all = lax.map(lambda one: normed(one, key_weight, key_gain), feats_all)
    values_all = lax.map(lambda one: jnp.dot(one, value_weight, preferred_element_type=jnp.float32).astype(jnp.bfloat16), feats_all)

    def one_frame(frame_pos):
        earlier = jnp.maximum(frame_pos - 1, 0)
        prev_keys = keys_all[earlier].reshape(NB, BLOCK, C)
        prev_values = values_all[earlier].reshape(NB, BLOCK, C)
        chosen = source_ids[frame_pos]
        key_set = jnp.concatenate([keys_all[frame_pos].reshape(NB, 1, BLOCK, C), prev_keys[chosen]], axis=1).reshape(NB, -1, C)
        value_set = jnp.concatenate([values_all[frame_pos].reshape(NB, 1, BLOCK, C), prev_values[chosen]], axis=1).reshape(NB, -1, C)
        slots = (jnp.arange(KSRC, dtype=jnp.int32)[None, :] < valid_counts[frame_pos][:, None]) & (frame_pos > 0)
        slot_mask = jnp.concatenate([jnp.ones((NB, 1), dtype=bool), slots], axis=1)
        mask = jnp.repeat(slot_mask, BLOCK, axis=1)
        mixed = attend(queries_all[frame_pos].reshape(NB, BLOCK, C), key_set, value_set, mask)
        result = feats_all[frame_pos].astype(jnp.float32) + jnp.dot(mixed, out_weight, preferred_element_type=jnp.float32)
        return result.astype(jnp.bfloat16).reshape(H, W, C)
    return lax.map(one_frame, jnp.arange(FRAMES, dtype=jnp.int32))
```

```python
import jax
import jax.numpy as jnp
from jax import lax
from jax.experimental import pallas as pl
from jax.experimental.pallas import tpu as pltpu
from jax.sharding import PartitionSpec as P

HD = 64
KSRC = 4
DISP = 2
GROUP = 4
LANES = GROUP * HD
LOG2E = 1.4426950408889634
F32 = jnp.float32
BF16 = jnp.bfloat16


def dot(a, b):
    return jnp.dot(a, b, preferred_element_type=F32)


def shift_columns(left, mid, right, width):
    count = mid.shape[0]
    col = lax.broadcasted_iota(jnp.int32, mid.shape, 0) % width
    return (
        mid
        + jnp.where(col == 0, 0.0, pltpu.roll(left, 1, 0))
        + jnp.where(col == width - 1, 0.0, pltpu.roll(right, count - 1, 0))
    )


def kernel(
    ids, valid, x, wc_hbm, wq_hbm, wk_hbm, wv_hbm, wo_hbm, bias, gq, gk,
    out,
    ext, wc, wq, wk, wv, wo, feats, reach, q, kdiag, vdiag, parts, acc, sums, mean, ones,
    local_sem, send_sem, recv_sem,
):
    rows, width, chans = x.shape
    groups = chans // LANES
    frame, band = lax.axis_index("frame"), lax.axis_index("row")
    frames, bands = lax.axis_size("frame"), lax.axis_size("row")
    has_prev, has_next = frame > 0, frame < frames - 1
    has_above, has_below = band > 0, band < bands - 1
    to_above, to_below, to_next = {"row": band - 1}, {"row": band + 1}, {"frame": frame + 1}

    def fetch(i, src, dst):
        return pltpu.make_async_copy(src, dst, local_sem.at[i])

    def send(i, src, dst, device):
        return pltpu.make_async_remote_copy(
            src_ref=src,
            dst_ref=dst,
            send_sem=send_sem.at[i],
            recv_sem=recv_sem.at[i],
            device_id=device,
            device_id_type=pl.DeviceIdType.MESH,
        )

    barrier = pltpu.get_barrier_semaphore()
    met = 0
    for there, device in (
        (has_above, to_above),
        (has_below, to_below),
        (has_prev, {"frame": frame - 1}),
        (has_next, to_next),
    ):
        met = met + there.astype(jnp.int32)

        @pl.when(there)
        def _():
            pl.semaphore_signal(
                barrier, inc=1, device_id=device, device_id_type=pl.DeviceIdType.MESH
            )

    load_x = fetch(0, x, ext.at[pl.ds(1, rows)])
    load_x.start()
    taps = [fetch(1 + b, wc_hbm.at[:, b], wc.at[b]) for b in range(3)]
    mats = [
        fetch(4 + i, src, dst)
        for i, (src, dst) in enumerate(
            ((wq_hbm, wq), (wk_hbm, wk), (wv_hbm, wv), (wo_hbm, wo))
        )
    ]
    for copy in taps:
        copy.start()

    kdiag[...] = jnp.zeros(kdiag.shape, BF16)
    vdiag[...] = jnp.zeros(vdiag.shape, BF16)
    row = lax.broadcasted_iota(jnp.int32, (LANES, LANES), 0) // HD
    col = lax.broadcasted_iota(jnp.int32, (LANES, LANES), 1) // HD
    mean[...] = jnp.where(row == col, 1.0 / HD, 0.0).astype(BF16)
    row = lax.broadcasted_iota(jnp.int32, (GROUP * width, LANES), 0) // width
    col = lax.broadcasted_iota(jnp.int32, (GROUP * width, LANES), 1) // HD
    ones[...] = jnp.where(row == col, 1.0, 0.0).astype(BF16)

    blank = jnp.zeros((width, chans), BF16)

    @pl.when(band == 0)
    def _():
        ext[0] = blank
        for i in range(DISP):
            reach[i] = blank

    @pl.when(band == bands - 1)
    def _():
        ext[rows + 1] = blank
        for i in range(DISP):
            reach[DISP + rows + i] = blank

    @pl.when(frame == 0)
    def _():
        for i in range(rows + 2 * DISP):
            reach[i] = blank

    pl.semaphore_wait(barrier, met)

    halo_up = send(0, x.at[0], ext.at[rows + 1], to_above)
    halo_down = send(1, x.at[rows - 1], ext.at[0], to_below)

    @pl.when(has_above)
    def _():
        halo_up.start()

    @pl.when(has_below)
    def _():
        halo_down.start()

    moves = [
        send(2 + r, feats.at[r], reach.at[DISP + r], to_next) for r in range(rows)
    ]
    relays = {}
    for i in range(DISP):
        relays[i] = (
            send(2 + rows + i, reach.at[DISP + i], reach.at[DISP + rows + i], to_above),
            has_above,
            has_below,
            DISP + rows + i,
        )
        r = rows - DISP + i
        relays[r] = (
            send(2 + rows + DISP + i, reach.at[DISP + r], reach.at[i], to_below),
            has_below,
            has_above,
            i,
        )

    chunks = [(1, rows - 2), (0, rows - 1)] + [
        tuple(range(r, min(r + 2, rows - DISP))) for r in range(DISP, rows - DISP, 2)
    ]

    load_x.wait()
    for i, chunk in enumerate(chunks):
        if i == 1:

            @pl.when(has_above)
            def _():
                halo_down.wait_recv()

            @pl.when(has_below)
            def _():
                halo_up.wait_recv()

        size = len(chunk) * width
        for b in range(3):
            if i == 0:
                taps[b].wait()
            window = jnp.concatenate(
                [jnp.concatenate([ext[r + a] for r in chunk], axis=0) for a in range(3)],
                axis=1,
            )
            parts[b, 0:size] = dot(window, wc[b].reshape(3 * chans, chans))
        total = shift_columns(parts[0, 0:size], parts[1, 0:size], parts[2, 0:size], width)
        total = (total + bias[...]).astype(BF16)
        for j, r in enumerate(chunk):
            feats[r] = total[j * width : (j + 1) * width]

        @pl.when(has_next)
        def _():
            for r in chunk:
                moves[r].start()

        if i == 0:
            for copy in mats:
                copy.start()

    def normed(flat, weight, gain):
        proj = dot(flat, weight[...])
        square = (proj * proj).astype(BF16)
        square = jnp.concatenate(
            [dot(square[:, g * LANES : (g + 1) * LANES], mean[...]) for g in range(groups)],
            axis=1,
        )
        return (proj * lax.rsqrt(square + 1e-06) * gain).astype(BF16)

    half = lax.broadcasted_iota(jnp.int32, (width, 2 * HD), 1) // HD

    def diagonal(ref, slot, value):
        for g in range(groups):
            for h in range(GROUP):
                lane = g * LANES + h // 2 * 2 * HD
                tile = value[:, lane : lane + 2 * HD]
                lane = h // 2 * 2 * HD
                ref[slot, g, h * width : (h + 1) * width, lane : lane + 2 * HD] = jnp.where(
                    half == h % 2, tile, jnp.zeros_like(tile)
                )

    def source(slot, flat):
        diagonal(kdiag, slot, normed(flat, wk, gk[...]))
        diagonal(vdiag, slot, dot(flat, wv[...]).astype(BF16))

    def attend(slot, first, last, counts):
        span = slice(first * width, last * width)
        for g in range(groups):
            lanes = slice(g * LANES, (g + 1) * LANES)
            expo = jnp.exp2(
                lax.dot_general(
                    q[span, lanes],
                    kdiag[slot, g],
                    (((1,), (1,)), ((), ())),
                    preferred_element_type=F32,
                )
            )
            if counts is not None:
                expo = jnp.concatenate(
                    [
                        expo[i * width : (i + 1) * width] * count
                        for i, count in enumerate(counts)
                    ],
                    axis=0,
                )
            mixed = dot(expo.astype(BF16), vdiag[slot, g])
            if counts is None:
                sums[g, span] = expo
                acc[span, lanes] = mixed
            else:
                sums[g, span] = sums[g, span] + expo
                acc[span, lanes] = acc[span, lanes] + mixed

    for copy in mats:
        copy.wait()
    flat = feats[...].reshape(rows * width, chans)
    q[...] = normed(flat, wq, gq[...] * (LOG2E * HD**-0.5))

    for n in range(rows):
        source(n % 2, feats[n])
        attend(n % 2, n, n + 1, None)

    live = has_prev.astype(jnp.int32)

    def named(n, place):
        count = 0
        for j in range(KSRC):
            here = ids[0, j, n] == band * rows + place - DISP
            count = count + (here & (j < valid[0, n])).astype(jnp.int32)
        return (count * live).astype(F32)

    def stage(k, place):
        first, last = max(place - 2 * DISP, 0), min(place, rows - 1) + 1
        source(k % 2, reach[place])
        attend(k % 2, first, last, [named(n, place) for n in range(first, last)])

    order = [r for chunk in chunks for r in chunk]
    k = 0
    late = []

    def pop(limit):
        nonlocal k
        while len(late) > limit:
            r = late.pop(0)
            relay, _, arriving, place = relays[r]

            @pl.when(has_prev & arriving)
            def _():
                relay.wait_recv()

            stage(k, place)
            k += 1

    for r in order:

        @pl.when(has_prev)
        def _():
            moves[r].wait_recv()

        if r in relays:
            relay, leaving, _, _ = relays[r]

            @pl.when(has_prev & leaving)
            def _():
                relay.start()

        stage(k, DISP + r)
        k += 1
        if r in relays:
            late.append(r)
        else:
            pop(0)
        pop(1)

    total = jnp.concatenate(
        [dot(sums[g].astype(BF16), ones[...]) for g in range(groups)], axis=1
    )
    mixed = (acc[...] * (1.0 / total)).astype(BF16)
    flat = feats[...].reshape(rows * width, chans).astype(F32)
    out[...] = (flat + dot(mixed, wo[...])).astype(BF16).reshape(rows, width, chans)

    @pl.when(has_above)
    def _():
        halo_up.wait_send()

    @pl.when(has_below)
    def _():
        halo_down.wait_send()

    @pl.when(has_next)
    def _():
        for copy in moves:
            copy.wait_send()

    for relay, leaving, _, _ in relays.values():

        @pl.when(has_prev & leaving)
        def _():
            relay.wait_send()


VM = pl.BlockSpec(memory_space=pltpu.VMEM)
SM = pl.BlockSpec(memory_space=pltpu.SMEM)
ANY = pl.BlockSpec(memory_space=pl.ANY)


def shards(x, wc, bias, wq, wk, wv, wo, gq, gk, source_ids, valid_counts):
    x = x[0]
    rows, width, chans = x.shape
    groups = chans // LANES
    square = pltpu.VMEM((chans, chans), BF16)

    def stack(count):
        return pltpu.VMEM((count, width, chans), BF16)

    links = 2 + rows + 2 * DISP
    out = pl.pallas_call(
        kernel,
        out_shape=jax.ShapeDtypeStruct((rows, width, chans), BF16),
        in_specs=[SM, SM] + [ANY] * 6 + [VM] * 3,
        out_specs=VM,
        scratch_shapes=[
            stack(rows + 2),
            pltpu.VMEM(wc.shape, BF16),
            square,
            square,
            square,
            square,
            stack(rows),
            stack(rows + 2 * DISP),
            pltpu.VMEM((rows * width, chans), BF16),
            pltpu.VMEM((2, groups, GROUP * width, LANES), BF16),
            pltpu.VMEM((2, groups, GROUP * width, LANES), BF16),
            pltpu.VMEM((3, 2 * width, chans), F32),
            pltpu.VMEM((rows * width, chans), F32),
            pltpu.VMEM((groups, rows * width, GROUP * width), F32),
            pltpu.VMEM((LANES, LANES), BF16),
            pltpu.VMEM((GROUP * width, LANES), BF16),
            pltpu.SemaphoreType.DMA((8,)),
            pltpu.SemaphoreType.DMA((links,)),
            pltpu.SemaphoreType.DMA((links,)),
        ],
        compiler_params=pltpu.CompilerParams(
            vmem_limit_bytes=56 * 2**20, collective_id=0, has_side_effects=True
        ),
    )(jnp.swapaxes(source_ids, 1, 2), valid_counts, x, wc, wq, wk, wv, wo, bias[None], gq[None], gk[None])
    return out[None]


def solution(mesh):
    return jax.shard_map(
        shards,
        mesh=mesh,
        in_specs=(P("frame", "row", None, None),)
        + (P(),) * 8
        + (P("frame", "row", None), P("frame", "row")),
        out_specs=P("frame", "row", None, None),
        check_vma=False,
    )
```

```python
import jax
import jax.numpy as jnp
from jax import lax
from jax.experimental import pallas as pl
from jax.experimental.pallas import tpu as pltpu
from jax.sharding import PartitionSpec as P

HD = 64
KSRC = 4
DISP = 2
GROUP = 4
LANES = GROUP * HD
LOG2E = 1.4426950408889634
F32 = jnp.float32
BF16 = jnp.bfloat16


def dot(a, b):
    return jnp.dot(a, b, preferred_element_type=F32)


def shift_columns(left, mid, right, width):
    count = mid.shape[0]
    col = lax.broadcasted_iota(jnp.int32, mid.shape, 0) % width
    return (
        mid
        + jnp.where(col == 0, 0.0, pltpu.roll(left, 1, 0))
        + jnp.where(col == width - 1, 0.0, pltpu.roll(right, count - 1, 0))
    )


def kernel(
    ids, valid, x, wc_hbm, wq_hbm, wk_hbm, wv_hbm, wo_hbm, bias, gq, gk,
    out,
    ext, wc, wq, wk, wv, wo, feats, reach, q, keys, values, kdiag, vdiag, parts, acc, sums, mean, ones,
    local_sem, send_sem, recv_sem,
):
    rows, width, chans = x.shape
    groups = chans // LANES
    frame, band = lax.axis_index("frame"), lax.axis_index("row")
    frames, bands = lax.axis_size("frame"), lax.axis_size("row")
    has_prev, has_next = frame > 0, frame < frames - 1
    has_above, has_below = band > 0, band < bands - 1
    to_above, to_below, to_next = {"row": band - 1}, {"row": band + 1}, {"frame": frame + 1}

    def fetch(i, src, dst):
        return pltpu.make_async_copy(src, dst, local_sem.at[i])

    def send(i, src, dst, device):
        return pltpu.make_async_remote_copy(
            src_ref=src,
            dst_ref=dst,
            send_sem=send_sem.at[i],
            recv_sem=recv_sem.at[i],
            device_id=device,
            device_id_type=pl.DeviceIdType.MESH,
        )

    barrier = pltpu.get_barrier_semaphore()
    met = 0
    for there, device in (
        (has_above, to_above),
        (has_below, to_below),
        (has_prev, {"frame": frame - 1}),
        (has_next, to_next),
    ):
        met = met + there.astype(jnp.int32)

        @pl.when(there)
        def _():
            pl.semaphore_signal(
                barrier, inc=1, device_id=device, device_id_type=pl.DeviceIdType.MESH
            )

    load_x = fetch(0, x, ext.at[pl.ds(1, rows)])
    load_x.start()
    taps = [fetch(1 + b, wc_hbm.at[:, b], wc.at[b]) for b in range(3)]
    mats = [
        fetch(4 + i, src, dst)
        for i, (src, dst) in enumerate(
            ((wq_hbm, wq), (wk_hbm, wk), (wv_hbm, wv), (wo_hbm, wo))
        )
    ]
    for copy in taps:
        copy.start()

    kdiag[...] = jnp.zeros(kdiag.shape, BF16)
    vdiag[...] = jnp.zeros(vdiag.shape, BF16)
    row = lax.broadcasted_iota(jnp.int32, (LANES, LANES), 0) // HD
    col = lax.broadcasted_iota(jnp.int32, (LANES, LANES), 1) // HD
    mean[...] = jnp.where(row == col, 1.0 / HD, 0.0).astype(BF16)
    row = lax.broadcasted_iota(jnp.int32, (GROUP * width, LANES), 0) // width
    col = lax.broadcasted_iota(jnp.int32, (GROUP * width, LANES), 1) // HD
    ones[...] = jnp.where(row == col, 1.0, 0.0).astype(BF16)

    blank = jnp.zeros((width, chans), BF16)

    @pl.when(band == 0)
    def _():
        ext[0] = blank
        for i in range(DISP):
            reach[i] = blank

    @pl.when(band == bands - 1)
    def _():
        ext[rows + 1] = blank
        for i in range(DISP):
            reach[DISP + rows + i] = blank

    @pl.when(frame == 0)
    def _():
        for i in range(rows + 2 * DISP):
            reach[i] = blank

    pl.semaphore_wait(barrier, met)

    halo_up = send(0, x.at[0], ext.at[rows + 1], to_above)
    halo_down = send(1, x.at[rows - 1], ext.at[0], to_below)

    @pl.when(has_above)
    def _():
        halo_up.start()

    @pl.when(has_below)
    def _():
        halo_down.start()

    moves = [
        send(2 + r, feats.at[r], reach.at[DISP + r], to_next) for r in range(rows)
    ]
    relays = {}
    for i in range(DISP):
        relays[i] = (
            send(2 + rows + i, reach.at[DISP + i], reach.at[DISP + rows + i], to_above),
            has_above,
            has_below,
            DISP + rows + i,
        )
        r = rows - DISP + i
        relays[r] = (
            send(2 + rows + DISP + i, reach.at[DISP + r], reach.at[i], to_below),
            has_below,
            has_above,
            i,
        )

    edges = [(1, rows - 2), (0, rows - 1)]
    inner = [tuple(range(r, min(r + 2, rows - DISP))) for r in range(DISP, rows - DISP, 2)]

    def convolve(chunk, first):
        size = len(chunk) * width
        for b in range(3):
            if first:
                taps[b].wait()
            window = jnp.concatenate(
                [jnp.concatenate([ext[r + a] for r in chunk], axis=0) for a in range(3)],
                axis=1,
            )
            parts[b, 0:size] = dot(window, wc[b].reshape(3 * chans, chans))
        total = shift_columns(parts[0, 0:size], parts[1, 0:size], parts[2, 0:size], width)
        total = (total + bias[...]).astype(BF16)
        for j, r in enumerate(chunk):
            feats[r] = total[j * width : (j + 1) * width]

    def forward(chunk):
        @pl.when(has_next)
        def _():
            for r in chunk:
                moves[r].start()

    def normed(flat, weight, gain):
        proj = dot(flat, weight[...])
        square = (proj * proj).astype(BF16)
        square = jnp.concatenate(
            [dot(square[:, g * LANES : (g + 1) * LANES], mean[...]) for g in range(groups)],
            axis=1,
        )
        return (proj * lax.rsqrt(square + 1e-06) * gain).astype(BF16)

    half = lax.broadcasted_iota(jnp.int32, (width, 2 * HD), 1) // HD

    def diagonal(ref, slot, value):
        for g in range(groups):
            for h in range(GROUP):
                lane = g * LANES + h // 2 * 2 * HD
                tile = value[:, lane : lane + 2 * HD]
                lane = h // 2 * 2 * HD
                ref[slot, g, h * width : (h + 1) * width, lane : lane + 2 * HD] = jnp.where(
                    half == h % 2, tile, jnp.zeros_like(tile)
                )

    def attend(slot, first, last, counts):
        span = slice(first * width, last * width)
        for g in range(groups):
            lanes = slice(g * LANES, (g + 1) * LANES)
            expo = jnp.exp2(
                lax.dot_general(
                    q[span, lanes],
                    kdiag[slot, g],
                    (((1,), (1,)), ((), ())),
                    preferred_element_type=F32,
                )
            )
            if counts is not None:
                expo = jnp.concatenate(
                    [
                        expo[i * width : (i + 1) * width] * count
                        for i, count in enumerate(counts)
                    ],
                    axis=0,
                )
            mixed = dot(expo.astype(BF16), vdiag[slot, g])
            if counts is None:
                sums[g, span] = expo
                acc[span, lanes] = mixed
            else:
                sums[g, span] = sums[g, span] + expo
                acc[span, lanes] = acc[span, lanes] + mixed

    def project(first, last):
        span = slice(first * width, last * width)
        flat = feats[first:last].reshape((last - first) * width, chans)
        q[span] = normed(flat, wq, gq[...] * (LOG2E * HD**-0.5))
        keys[span] = normed(flat, wk, gk[...])
        values[span] = dot(flat, wv[...]).astype(BF16)

    load_x.wait()
    convolve(edges[0], True)
    forward(edges[0])
    for copy in mats:
        copy.start()
    for chunk in inner:
        convolve(chunk, False)
    for copy in mats:
        copy.wait()
    project(1, rows - 1)

    @pl.when(has_above)
    def _():
        halo_down.wait_recv()

    @pl.when(has_below)
    def _():
        halo_up.wait_recv()

    convolve(edges[1], False)
    forward(edges[1])
    for chunk in inner:
        forward(chunk)
    for r in edges[1]:
        project(r, r + 1)
    slots = kdiag.shape[0]
    for n in range(rows):
        span = slice(n * width, (n + 1) * width)
        diagonal(kdiag, n % slots, keys[span])
        diagonal(vdiag, n % slots, values[span])
        attend(n % slots, n, n + 1, None)

    live = has_prev.astype(jnp.int32)

    def named(n, place):
        count = 0
        for j in range(KSRC):
            here = ids[0, j, n] == band * rows + place - DISP
            count = count + (here & (j < valid[0, n])).astype(jnp.int32)
        return (count * live).astype(F32)

    def stages(places, k):
        flat = jnp.concatenate([reach[place] for place in places], axis=0)
        key = normed(flat, wk, gk[...])
        value = dot(flat, wv[...]).astype(BF16)
        for i, place in enumerate(places):
            slot = (k + i) % slots
            first, last = max(place - 2 * DISP, 0), min(place, rows - 1) + 1
            diagonal(kdiag, slot, key[i * width : (i + 1) * width])
            diagonal(vdiag, slot, value[i * width : (i + 1) * width])
            attend(slot, first, last, [named(n, place) for n in range(first, last)])

    late = []
    for i, r in enumerate([r for chunk in edges + inner for r in chunk]):

        @pl.when(has_prev)
        def _():
            moves[r].wait_recv()

        if r in relays:
            relay, leaving, _, _ = relays[r]

            @pl.when(has_prev & leaving)
            def _():
                relay.start()

        places = [DISP + r]
        if late:
            relay, arriving, place = late.pop(0)

            @pl.when(has_prev & arriving)
            def _():
                relay.wait_recv()

            places.append(place)
        stages(places, 2 * i)
        if r in relays:
            relay, _, arriving, place = relays[r]
            late.append((relay, arriving, place))

    total = jnp.concatenate(
        [dot(sums[g].astype(BF16), ones[...]) for g in range(groups)], axis=1
    )
    mixed = (acc[...] * (1.0 / total)).astype(BF16)
    flat = feats[...].reshape(rows * width, chans).astype(F32)
    out[...] = (flat + dot(mixed, wo[...])).astype(BF16).reshape(rows, width, chans)

    @pl.when(has_above)
    def _():
        halo_up.wait_send()

    @pl.when(has_below)
    def _():
        halo_down.wait_send()

    @pl.when(has_next)
    def _():
        for copy in moves:
            copy.wait_send()

    for relay, leaving, _, _ in relays.values():

        @pl.when(has_prev & leaving)
        def _():
            relay.wait_send()


VM = pl.BlockSpec(memory_space=pltpu.VMEM)
SM = pl.BlockSpec(memory_space=pltpu.SMEM)
ANY = pl.BlockSpec(memory_space=pl.ANY)


def shards(x, wc, bias, wq, wk, wv, wo, gq, gk, source_ids, valid_counts):
    x = x[0]
    rows, width, chans = x.shape
    groups = chans // LANES
    square = pltpu.VMEM((chans, chans), BF16)

    def stack(count):
        return pltpu.VMEM((count, width, chans), BF16)

    links = 2 + rows + 2 * DISP
    out = pl.pallas_call(
        kernel,
        out_shape=jax.ShapeDtypeStruct((rows, width, chans), BF16),
        in_specs=[SM, SM] + [ANY] * 6 + [VM] * 3,
        out_specs=VM,
        scratch_shapes=[
            stack(rows + 2),
            pltpu.VMEM(wc.shape, BF16),
            square,
            square,
            square,
            square,
            stack(rows),
            stack(rows + 2 * DISP),
            pltpu.VMEM((rows * width, chans), BF16),
            pltpu.VMEM((rows * width, chans), BF16),
            pltpu.VMEM((rows * width, chans), BF16),
            pltpu.VMEM((4, groups, GROUP * width, LANES), BF16),
            pltpu.VMEM((4, groups, GROUP * width, LANES), BF16),
            pltpu.VMEM((3, 2 * width, chans), F32),
            pltpu.VMEM((rows * width, chans), F32),
            pltpu.VMEM((groups, rows * width, GROUP * width), F32),
            pltpu.VMEM((LANES, LANES), BF16),
            pltpu.VMEM((GROUP * width, LANES), BF16),
            pltpu.SemaphoreType.DMA((8,)),
            pltpu.SemaphoreType.DMA((links,)),
            pltpu.SemaphoreType.DMA((links,)),
        ],
        compiler_params=pltpu.CompilerParams(
            vmem_limit_bytes=56 * 2**20, collective_id=0, has_side_effects=True
        ),
    )(jnp.swapaxes(source_ids, 1, 2), valid_counts, x, wc, wq, wk, wv, wo, bias[None], gq[None], gk[None])
    return out[None]


def solution(mesh):
    return jax.shard_map(
        shards,
        mesh=mesh,
        in_specs=(P("frame", "row", None, None),)
        + (P(),) * 8
        + (P("frame", "row", None), P("frame", "row")),
        out_specs=P("frame", "row", None, None),
        check_vma=False,
    )
```

```python
import jax
import jax.numpy as jnp
from jax import lax
from jax.experimental import pallas as pl
from jax.experimental.pallas import tpu as pltpu
from jax.sharding import PartitionSpec as P

HD = 64
KSRC = 4
DISP = 2
GROUP = 4
LANES = GROUP * HD
LOG2E = 1.4426950408889634
F32 = jnp.float32
BF16 = jnp.bfloat16


def dot(a, b):
    return jnp.dot(a, b, preferred_element_type=F32)


def shift_columns(left, mid, right, width):
    count = mid.shape[0]
    col = lax.broadcasted_iota(jnp.int32, mid.shape, 0) % width
    return (
        mid
        + jnp.where(col == 0, 0.0, pltpu.roll(left, 1, 0))
        + jnp.where(col == width - 1, 0.0, pltpu.roll(right, count - 1, 0))
    )


def kernel(
    ids, valid, x, wc_hbm, wq_hbm, wk_hbm, wv_hbm, bias, gq, gk,
    feats, attended,
    ext, wc, wq, wk, wv, reach, q, keys, values, kdiag, vdiag, parts, acc, sums, mean, ones,
    local_sem, send_sem, recv_sem,
):
    rows, width, chans = x.shape
    groups = chans // LANES
    frame, band = lax.axis_index("frame"), lax.axis_index("row")
    frames, bands = lax.axis_size("frame"), lax.axis_size("row")
    has_prev, has_next = frame > 0, frame < frames - 1
    has_above, has_below = band > 0, band < bands - 1
    to_above, to_below, to_next = {"row": band - 1}, {"row": band + 1}, {"frame": frame + 1}

    def fetch(i, src, dst):
        return pltpu.make_async_copy(src, dst, local_sem.at[i])

    def send(i, src, dst, device):
        return pltpu.make_async_remote_copy(
            src_ref=src,
            dst_ref=dst,
            send_sem=send_sem.at[i],
            recv_sem=recv_sem.at[i],
            device_id=device,
            device_id_type=pl.DeviceIdType.MESH,
        )

    barrier = pltpu.get_barrier_semaphore()
    met = 0
    for there, device in (
        (has_above, to_above),
        (has_below, to_below),
        (has_prev, {"frame": frame - 1}),
        (has_next, to_next),
    ):
        met = met + there.astype(jnp.int32)

        @pl.when(there)
        def _():
            pl.semaphore_signal(
                barrier, inc=1, device_id=device, device_id_type=pl.DeviceIdType.MESH
            )

    load_x = fetch(0, x, ext.at[pl.ds(1, rows)])
    load_x.start()
    taps = [fetch(1 + b, wc_hbm.at[:, b], wc.at[b]) for b in range(3)]
    mats = [
        fetch(4 + i, src, dst)
        for i, (src, dst) in enumerate(
            ((wq_hbm, wq), (wk_hbm, wk), (wv_hbm, wv))
        )
    ]
    for copy in taps:
        copy.start()

    kdiag[...] = jnp.zeros(kdiag.shape, BF16)
    vdiag[...] = jnp.zeros(vdiag.shape, BF16)
    row = lax.broadcasted_iota(jnp.int32, (LANES, LANES), 0) // HD
    col = lax.broadcasted_iota(jnp.int32, (LANES, LANES), 1) // HD
    mean[...] = jnp.where(row == col, 1.0 / HD, 0.0).astype(BF16)
    row = lax.broadcasted_iota(jnp.int32, (GROUP * width, LANES), 0) // width
    col = lax.broadcasted_iota(jnp.int32, (GROUP * width, LANES), 1) // HD
    ones[...] = jnp.where(row == col, 1.0, 0.0).astype(BF16)

    blank = jnp.zeros((width, chans), BF16)

    @pl.when(band == 0)
    def _():
        ext[0] = blank
        for i in range(DISP):
            reach[i] = blank

    @pl.when(band == bands - 1)
    def _():
        ext[rows + 1] = blank
        for i in range(DISP):
            reach[DISP + rows + i] = blank

    @pl.when(frame == 0)
    def _():
        for i in range(rows + 2 * DISP):
            reach[i] = blank

    pl.semaphore_wait(barrier, met)

    halo_up = send(0, x.at[0], ext.at[rows + 1], to_above)
    halo_down = send(1, x.at[rows - 1], ext.at[0], to_below)

    @pl.when(has_above)
    def _():
        halo_up.start()

    @pl.when(has_below)
    def _():
        halo_down.start()

    moves = [
        send(2 + r, feats.at[r], reach.at[DISP + r], to_next) for r in range(rows)
    ]
    relays = {}
    for i in range(DISP):
        relays[i] = (
            send(2 + rows + i, reach.at[DISP + i], reach.at[DISP + rows + i], to_above),
            has_above,
            has_below,
            DISP + rows + i,
        )
        r = rows - DISP + i
        relays[r] = (
            send(2 + rows + DISP + i, reach.at[DISP + r], reach.at[i], to_below),
            has_below,
            has_above,
            i,
        )

    edges = [(1, rows - 2), (0, rows - 1)]
    inner = [tuple(range(r, min(r + 2, rows - DISP))) for r in range(DISP, rows - DISP, 2)]

    def convolve(chunk, first):
        size = len(chunk) * width
        for b in range(3):
            if first:
                taps[b].wait()
            window = jnp.concatenate(
                [jnp.concatenate([ext[r + a] for r in chunk], axis=0) for a in range(3)],
                axis=1,
            )
            parts[b, 0:size] = dot(window, wc[b].reshape(3 * chans, chans))
        total = shift_columns(parts[0, 0:size], parts[1, 0:size], parts[2, 0:size], width)
        total = (total + bias[...]).astype(BF16)
        for j, r in enumerate(chunk):
            feats[r] = total[j * width : (j + 1) * width]

    def forward(chunk):
        @pl.when(has_next)
        def _():
            for r in chunk:
                moves[r].start()

    def normed(flat, weight, gain):
        proj = dot(flat, weight[...])
        square = (proj * proj).astype(BF16)
        square = jnp.concatenate(
            [dot(square[:, g * LANES : (g + 1) * LANES], mean[...]) for g in range(groups)],
            axis=1,
        )
        return (proj * lax.rsqrt(square + 1e-06) * gain).astype(BF16)

    half = lax.broadcasted_iota(jnp.int32, (width, 2 * HD), 1) // HD

    def diagonal(ref, slot, value):
        for g in range(groups):
            for h in range(GROUP):
                lane = g * LANES + h // 2 * 2 * HD
                tile = value[:, lane : lane + 2 * HD]
                lane = h // 2 * 2 * HD
                ref[slot, g, h * width : (h + 1) * width, lane : lane + 2 * HD] = jnp.where(
                    half == h % 2, tile, jnp.zeros_like(tile)
                )

    def attend(slot, first, last, counts):
        span = slice(first * width, last * width)
        probs = []
        for g in range(groups):
            lanes = slice(g * LANES, (g + 1) * LANES)
            expo = jnp.exp2(
                lax.dot_general(
                    q[span, lanes],
                    kdiag[slot, g],
                    (((1,), (1,)), ((), ())),
                    preferred_element_type=F32,
                )
            )
            if counts is None:
                sums[g, span] = expo
            else:
                expo = jnp.concatenate(
                    [
                        expo[i * width : (i + 1) * width] * count
                        for i, count in enumerate(counts)
                    ],
                    axis=0,
                )
                sums[g, span] = sums[g, span] + expo
            probs.append(expo.astype(BF16))
        mixed = [dot(probs[g], vdiag[slot, g]) for g in range(groups)]
        for g in range(groups):
            lanes = slice(g * LANES, (g + 1) * LANES)
            if counts is None:
                acc[span, lanes] = mixed[g]
            else:
                acc[span, lanes] = acc[span, lanes] + mixed[g]

    def project(first, last):
        span = slice(first * width, last * width)
        flat = feats[first:last].reshape((last - first) * width, chans)
        q[span] = normed(flat, wq, gq[...] * (LOG2E * HD**-0.5))
        keys[span] = normed(flat, wk, gk[...])
        values[span] = dot(flat, wv[...]).astype(BF16)

    load_x.wait()
    convolve(edges[0], True)
    forward(edges[0])
    for copy in mats:
        copy.start()
    for chunk in inner:
        convolve(chunk, False)
    for copy in mats:
        copy.wait()
    project(1, rows - 1)

    @pl.when(has_above)
    def _():
        halo_down.wait_recv()

    @pl.when(has_below)
    def _():
        halo_up.wait_recv()

    convolve(edges[1], False)
    forward(edges[1])
    for chunk in inner:
        forward(chunk)
    for r in edges[1]:
        project(r, r + 1)
    slots = kdiag.shape[0]
    for n in range(rows):
        span = slice(n * width, (n + 1) * width)
        diagonal(kdiag, n % slots, keys[span])
        diagonal(vdiag, n % slots, values[span])
        attend(n % slots, n, n + 1, None)

    live = has_prev.astype(jnp.int32)

    def named(n, place):
        count = 0
        for j in range(KSRC):
            here = ids[0, j, n] == band * rows + place - DISP
            count = count + (here & (j < valid[0, n])).astype(jnp.int32)
        return (count * live).astype(F32)

    def stages(places, k):
        flat = jnp.concatenate([reach[place] for place in places], axis=0)
        key = normed(flat, wk, gk[...])
        value = dot(flat, wv[...]).astype(BF16)
        for i, place in enumerate(places):
            slot = (k + i) % slots
            first, last = max(place - 2 * DISP, 0), min(place, rows - 1) + 1
            diagonal(kdiag, slot, key[i * width : (i + 1) * width])
            diagonal(vdiag, slot, value[i * width : (i + 1) * width])
            attend(slot, first, last, [named(n, place) for n in range(first, last)])

    late = []
    for i, r in enumerate([r for chunk in edges + inner for r in chunk]):

        @pl.when(has_prev)
        def _():
            moves[r].wait_recv()

        if r in relays:
            relay, leaving, _, _ = relays[r]

            @pl.when(has_prev & leaving)
            def _():
                relay.start()

        places = [DISP + r]
        if late:
            relay, arriving, place = late.pop(0)

            @pl.when(has_prev & arriving)
            def _():
                relay.wait_recv()

            places.append(place)
        stages(places, 2 * i)
        if r in relays:
            relay, _, arriving, place = relays[r]
            late.append((relay, arriving, place))

    total = jnp.concatenate(
        [dot(sums[g].astype(BF16), ones[...]) for g in range(groups)], axis=1
    )
    attended[...] = (acc[...] * (1.0 / total)).astype(BF16).reshape(rows, width, chans)

    @pl.when(has_above)
    def _():
        halo_up.wait_send()

    @pl.when(has_below)
    def _():
        halo_down.wait_send()

    @pl.when(has_next)
    def _():
        for copy in moves:
            copy.wait_send()

    for relay, leaving, _, _ in relays.values():

        @pl.when(has_prev & leaving)
        def _():
            relay.wait_send()


def join(feats, attended, wo, out, stage, sem):
    rows, width, chans = feats.shape
    copies = []
    for r in range(rows):
        stage[r] = (feats[r].astype(F32) + dot(attended[r], wo[...])).astype(BF16)
        copies.append(pltpu.make_async_copy(stage.at[r], out.at[r], sem.at[r]))
        copies[r].start()
    for copy in copies:
        copy.wait()


VM = pl.BlockSpec(memory_space=pltpu.VMEM)
SM = pl.BlockSpec(memory_space=pltpu.SMEM)
ANY = pl.BlockSpec(memory_space=pltpu.HBM)


def shards(x, wc, bias, wq, wk, wv, wo, gq, gk, source_ids, valid_counts):
    x = x[0]
    rows, width, chans = x.shape
    groups = chans // LANES
    square = pltpu.VMEM((chans, chans), BF16)

    def stack(count):
        return pltpu.VMEM((count, width, chans), BF16)

    links = 2 + rows + 2 * DISP
    shape = jax.ShapeDtypeStruct((rows, width, chans), BF16)
    feats, attended = pl.pallas_call(
        kernel,
        out_shape=(pltpu.VMEM(shape.shape, BF16), pltpu.VMEM(shape.shape, BF16)),
        in_specs=[SM, SM] + [ANY] * 5 + [VM] * 3,
        out_specs=(VM, VM),
        scratch_shapes=[
            stack(rows + 2),
            pltpu.VMEM(wc.shape, BF16),
            square,
            square,
            square,
            stack(rows + 2 * DISP),
            pltpu.VMEM((rows * width, chans), BF16),
            pltpu.VMEM((rows * width, chans), BF16),
            pltpu.VMEM((rows * width, chans), BF16),
            pltpu.VMEM((4, groups, GROUP * width, LANES), BF16),
            pltpu.VMEM((4, groups, GROUP * width, LANES), BF16),
            pltpu.VMEM((3, 2 * width, chans), F32),
            pltpu.VMEM((rows * width, chans), F32),
            pltpu.VMEM((groups, rows * width, GROUP * width), F32),
            pltpu.VMEM((LANES, LANES), BF16),
            pltpu.VMEM((GROUP * width, LANES), BF16),
            pltpu.SemaphoreType.DMA((8,)),
            pltpu.SemaphoreType.DMA((links,)),
            pltpu.SemaphoreType.DMA((links,)),
        ],
        compiler_params=pltpu.CompilerParams(
            vmem_limit_bytes=56 * 2**20, collective_id=0, has_side_effects=True
        ),
    )(jnp.swapaxes(source_ids, 1, 2), valid_counts, x, wc, wq, wk, wv, bias[None], gq[None], gk[None])
    out = pl.pallas_call(
        join,
        out_shape=shape,
        in_specs=[VM] * 3,
        out_specs=ANY,
        scratch_shapes=[
            pltpu.VMEM((rows, width, chans), BF16),
            pltpu.SemaphoreType.DMA((rows,)),
        ],
        compiler_params=pltpu.CompilerParams(vmem_limit_bytes=12 * 2**20),
    )(feats, attended, wo)
    return out[None]


def solution(mesh):
    return jax.shard_map(
        shards,
        mesh=mesh,
        in_specs=(P("frame", "row", None, None),)
        + (P(),) * 8
        + (P("frame", "row", None), P("frame", "row")),
        out_specs=P("frame", "row", None, None),
        check_vma=False,
    )
```

```python
import jax
import jax.numpy as jnp
from jax import lax
from jax.experimental import pallas as pl
from jax.experimental.pallas import tpu as pltpu
from jax.sharding import PartitionSpec as P

HD = 64
KSRC = 4
DISP = 2
GROUP = 4
LANES = GROUP * HD
LOG2E = 1.4426950408889634
F32 = jnp.float32
BF16 = jnp.bfloat16


def dot(a, b):
    return jnp.dot(a, b, preferred_element_type=F32)


def shift_columns(left, mid, right, width):
    count = mid.shape[0]
    col = lax.broadcasted_iota(jnp.int32, mid.shape, 0) % width
    return (
        mid
        + jnp.where(col == 0, 0.0, pltpu.roll(left, 1, 0))
        + jnp.where(col == width - 1, 0.0, pltpu.roll(right, count - 1, 0))
    )


def kernel(
    ids, valid, x, wc_hbm, wq_hbm, wk_hbm, wv_hbm, bias, gq, gk,
    feats, attended,
    ext, wc, wq, wk, wv, reach, q, keys, values, kdiag, vdiag, parts, acc, sums, mean,
    local_sem, send_sem, recv_sem,
):
    rows, width, chans = x.shape
    groups = chans // LANES
    frame, band = lax.axis_index("frame"), lax.axis_index("row")
    frames, bands = lax.axis_size("frame"), lax.axis_size("row")
    has_prev, has_next = frame > 0, frame < frames - 1
    has_above, has_below = band > 0, band < bands - 1
    to_above, to_below, to_next = {"row": band - 1}, {"row": band + 1}, {"frame": frame + 1}

    def fetch(i, src, dst):
        return pltpu.make_async_copy(src, dst, local_sem.at[i])

    def send(i, src, dst, device):
        return pltpu.make_async_remote_copy(
            src_ref=src,
            dst_ref=dst,
            send_sem=send_sem.at[i],
            recv_sem=recv_sem.at[i],
            device_id=device,
            device_id_type=pl.DeviceIdType.MESH,
        )

    barrier = pltpu.get_barrier_semaphore()
    met = 0
    for there, device in (
        (has_above, to_above),
        (has_below, to_below),
        (has_prev, {"frame": frame - 1}),
        (has_next, to_next),
    ):
        met = met + there.astype(jnp.int32)

        @pl.when(there)
        def _():
            pl.semaphore_signal(
                barrier, inc=1, device_id=device, device_id_type=pl.DeviceIdType.MESH
            )

    load_x = fetch(0, x, ext.at[pl.ds(1, rows)])
    load_x.start()
    taps = [fetch(1 + b, wc_hbm.at[:, b], wc.at[b]) for b in range(3)]
    mats = [
        fetch(4 + i, src, dst)
        for i, (src, dst) in enumerate(
            ((wq_hbm, wq), (wk_hbm, wk), (wv_hbm, wv))
        )
    ]
    for copy in taps:
        copy.start()

    kdiag[...] = jnp.zeros(kdiag.shape, BF16)
    vdiag[...] = jnp.zeros(vdiag.shape, BF16)
    row = lax.broadcasted_iota(jnp.int32, (LANES, LANES), 0) // HD
    col = lax.broadcasted_iota(jnp.int32, (LANES, LANES), 1) // HD
    mean[...] = jnp.where(row == col, 1.0 / HD, 0.0).astype(BF16)

    blank = jnp.zeros((width, chans), BF16)

    @pl.when(band == 0)
    def _():
        ext[0] = blank
        for i in range(DISP):
            reach[i] = blank

    @pl.when(band == bands - 1)
    def _():
        ext[rows + 1] = blank
        for i in range(DISP):
            reach[DISP + rows + i] = blank

    @pl.when(frame == 0)
    def _():
        for i in range(rows + 2 * DISP):
            reach[i] = blank

    pl.semaphore_wait(barrier, met)

    halo_up = send(0, x.at[0], ext.at[rows + 1], to_above)
    halo_down = send(1, x.at[rows - 1], ext.at[0], to_below)

    @pl.when(has_above)
    def _():
        halo_up.start()

    @pl.when(has_below)
    def _():
        halo_down.start()

    moves = [
        send(2 + r, feats.at[r], reach.at[DISP + r], to_next) for r in range(rows)
    ]
    relays = {}
    for i in range(DISP):
        relays[i] = (
            send(2 + rows + i, reach.at[DISP + i], reach.at[DISP + rows + i], to_above),
            has_above,
            has_below,
            DISP + rows + i,
        )
        r = rows - DISP + i
        relays[r] = (
            send(2 + rows + DISP + i, reach.at[DISP + r], reach.at[i], to_below),
            has_below,
            has_above,
            i,
        )

    edges = [(1, rows - 2), (0, rows - 1)]
    inner = [tuple(range(r, min(r + 2, rows - DISP))) for r in range(DISP, rows - DISP, 2)]

    def convolve(chunk, first):
        size = len(chunk) * width
        for b in range(3):
            if first:
                taps[b].wait()
            window = jnp.concatenate(
                [jnp.concatenate([ext[r + a] for r in chunk], axis=0) for a in range(3)],
                axis=1,
            )
            parts[b, 0:size] = dot(window, wc[b].reshape(3 * chans, chans))
        total = shift_columns(parts[0, 0:size], parts[1, 0:size], parts[2, 0:size], width)
        total = (total + bias[...]).astype(BF16)
        for j, r in enumerate(chunk):
            feats[r] = total[j * width : (j + 1) * width]

    def forward(chunk):
        @pl.when(has_next)
        def _():
            for r in chunk:
                moves[r].start()

    def normed(flat, weight, gain):
        proj = dot(flat, weight[...])
        square = (proj * proj).astype(BF16)
        square = jnp.concatenate(
            [dot(square[:, g * LANES : (g + 1) * LANES], mean[...]) for g in range(groups)],
            axis=1,
        )
        return (proj * lax.rsqrt(square + 1e-06) * gain).astype(BF16)

    half = lax.broadcasted_iota(jnp.int32, (width, 2 * HD), 1) // HD

    def diagonal(ref, slot, value):
        for g in range(groups):
            for h in range(GROUP):
                lane = g * LANES + h // 2 * 2 * HD
                tile = value[:, lane : lane + 2 * HD]
                lane = h // 2 * 2 * HD
                ref[slot, g, h * width : (h + 1) * width, lane : lane + 2 * HD] = jnp.where(
                    half == h % 2, tile, jnp.zeros_like(tile)
                )

    def attend(slot, first, last, counts):
        span = slice(first * width, last * width)
        probs = []
        for g in range(groups):
            lanes = slice(g * LANES, (g + 1) * LANES)
            expo = jnp.exp2(
                lax.dot_general(
                    q[span, lanes],
                    kdiag[slot, g],
                    (((1,), (1,)), ((), ())),
                    preferred_element_type=F32,
                )
            )
            if counts is None:
                sums[g, span] = expo
            else:
                expo = jnp.concatenate(
                    [
                        expo[i * width : (i + 1) * width] * count
                        for i, count in enumerate(counts)
                    ],
                    axis=0,
                )
                sums[g, span] = sums[g, span] + expo
            probs.append(expo.astype(BF16))
        mixed = [dot(probs[g], vdiag[slot, g]) for g in range(groups)]
        for g in range(groups):
            lanes = slice(g * LANES, (g + 1) * LANES)
            if counts is None:
                acc[span, lanes] = mixed[g]
            else:
                acc[span, lanes] = acc[span, lanes] + mixed[g]

    def project(first, last):
        span = slice(first * width, last * width)
        flat = feats[first:last].reshape((last - first) * width, chans)
        q[span] = normed(flat, wq, gq[...] * (LOG2E * HD**-0.5))
        keys[span] = normed(flat, wk, gk[...])
        values[span] = dot(flat, wv[...]).astype(BF16)

    load_x.wait()
    convolve(edges[0], True)
    forward(edges[0])
    for copy in mats:
        copy.start()
    for chunk in inner:
        convolve(chunk, False)
    for copy in mats:
        copy.wait()
    project(1, rows - 1)

    @pl.when(has_above)
    def _():
        halo_down.wait_recv()

    @pl.when(has_below)
    def _():
        halo_up.wait_recv()

    convolve(edges[1], False)
    forward(edges[1])
    for chunk in inner:
        forward(chunk)
    for r in edges[1]:
        project(r, r + 1)
    slots = kdiag.shape[0]
    for n in range(rows):
        span = slice(n * width, (n + 1) * width)
        diagonal(kdiag, n % slots, keys[span])
        diagonal(vdiag, n % slots, values[span])
        attend(n % slots, n, n + 1, None)

    live = has_prev.astype(jnp.int32)

    def named(n, place):
        count = 0
        for j in range(KSRC):
            here = ids[0, j, n] == band * rows + place - DISP
            count = count + (here & (j < valid[0, n])).astype(jnp.int32)
        return (count * live).astype(F32)

    def stages(places, k):
        flat = jnp.concatenate([reach[place] for place in places], axis=0)
        key = normed(flat, wk, gk[...])
        value = dot(flat, wv[...]).astype(BF16)
        for i, place in enumerate(places):
            slot = (k + i) % slots
            first, last = max(place - 2 * DISP, 0), min(place, rows - 1) + 1
            diagonal(kdiag, slot, key[i * width : (i + 1) * width])
            diagonal(vdiag, slot, value[i * width : (i + 1) * width])
            attend(slot, first, last, [named(n, place) for n in range(first, last)])

    side = lax.broadcasted_iota(jnp.int32, (width, 2 * HD), 1) // HD

    def finish(n):
        span = slice(n * width, (n + 1) * width)
        for g in range(groups):
            total = [
                jnp.sum(sums[g, span, h * width : (h + 1) * width], axis=1, keepdims=True)
                for h in range(GROUP)
            ]
            for h in range(0, GROUP, 2):
                lanes = slice(g * LANES + h * HD, g * LANES + (h + 2) * HD)
                inverse = 1.0 / jnp.where(side == 0, total[h], total[h + 1])
                attended[n, :, lanes] = (acc[span, lanes] * inverse).astype(BF16)

    steps = []
    late = []
    for r in [r for chunk in edges + inner for r in chunk]:
        step = [(moves[r], None, DISP + r, r)]
        if len(late) > 1:
            step.append(late.pop(0))
        steps.append(step)
        if r in relays:
            relay, _, arriving, place = relays[r]
            late.append((relay, arriving, place, None))
    steps[-1:-1] = [[entry] for entry in late]

    left = [2 * DISP + 1] * rows
    k = 0
    for step in steps:
        for copy, arriving, _, r in step:

            @pl.when(has_prev if arriving is None else has_prev & arriving)
            def _():
                copy.wait_recv()

            if r in relays:
                relay, leaving, _, _ = relays[r]

                @pl.when(has_prev & leaving)
                def _():
                    relay.start()

        places = [place for _, _, place, _ in step]
        stages(places, k)
        k += len(places)
        for place in places:
            for n in range(max(place - 2 * DISP, 0), min(place, rows - 1) + 1):
                left[n] -= 1
                if left[n] == 0:
                    finish(n)

    @pl.when(has_above)
    def _():
        halo_up.wait_send()

    @pl.when(has_below)
    def _():
        halo_down.wait_send()

    @pl.when(has_next)
    def _():
        for copy in moves:
            copy.wait_send()

    for relay, leaving, _, _ in relays.values():

        @pl.when(has_prev & leaving)
        def _():
            relay.wait_send()


def join(feats, attended, wo, out, stage, sem):
    rows, width, chans = feats.shape
    copies = []
    for r in range(rows):
        stage[r] = (feats[r].astype(F32) + dot(attended[r], wo[...])).astype(BF16)
        copies.append(pltpu.make_async_copy(stage.at[r], out.at[r], sem.at[r]))
        copies[r].start()
    for copy in copies:
        copy.wait()


VM = pl.BlockSpec(memory_space=pltpu.VMEM)
SM = pl.BlockSpec(memory_space=pltpu.SMEM)
ANY = pl.BlockSpec(memory_space=pltpu.HBM)


def shards(x, wc, bias, wq, wk, wv, wo, gq, gk, source_ids, valid_counts):
    x = x[0]
    rows, width, chans = x.shape
    groups = chans // LANES
    square = pltpu.VMEM((chans, chans), BF16)

    def stack(count):
        return pltpu.VMEM((count, width, chans), BF16)

    links = 2 + rows + 2 * DISP
    shape = jax.ShapeDtypeStruct((rows, width, chans), BF16)
    feats, attended = pl.pallas_call(
        kernel,
        out_shape=(pltpu.VMEM(shape.shape, BF16), pltpu.VMEM(shape.shape, BF16)),
        in_specs=[SM, SM] + [ANY] * 5 + [VM] * 3,
        out_specs=(VM, VM),
        scratch_shapes=[
            stack(rows + 2),
            pltpu.VMEM(wc.shape, BF16),
            square,
            square,
            square,
            stack(rows + 2 * DISP),
            pltpu.VMEM((rows * width, chans), BF16),
            pltpu.VMEM((rows * width, chans), BF16),
            pltpu.VMEM((rows * width, chans), BF16),
            pltpu.VMEM((4, groups, GROUP * width, LANES), BF16),
            pltpu.VMEM((4, groups, GROUP * width, LANES), BF16),
            pltpu.VMEM((3, 2 * width, chans), F32),
            pltpu.VMEM((rows * width, chans), F32),
            pltpu.VMEM((groups, rows * width, GROUP * width), F32),
            pltpu.VMEM((LANES, LANES), BF16),
            pltpu.SemaphoreType.DMA((8,)),
            pltpu.SemaphoreType.DMA((links,)),
            pltpu.SemaphoreType.DMA((links,)),
        ],
        compiler_params=pltpu.CompilerParams(
            vmem_limit_bytes=56 * 2**20, collective_id=0, has_side_effects=True
        ),
    )(jnp.swapaxes(source_ids, 1, 2), valid_counts, x, wc, wq, wk, wv, bias[None], gq[None], gk[None])
    out = pl.pallas_call(
        join,
        out_shape=shape,
        in_specs=[VM] * 3,
        out_specs=ANY,
        scratch_shapes=[
            pltpu.VMEM((rows, width, chans), BF16),
            pltpu.SemaphoreType.DMA((rows,)),
        ],
        compiler_params=pltpu.CompilerParams(vmem_limit_bytes=12 * 2**20),
    )(feats, attended, wo)
    return out[None]


def solution(mesh):
    return jax.shard_map(
        shards,
        mesh=mesh,
        in_specs=(P("frame", "row", None, None),)
        + (P(),) * 8
        + (P("frame", "row", None), P("frame", "row")),
        out_specs=P("frame", "row", None, None),
        check_vma=False,
    )
```

```python
import jax
import jax.numpy as jnp
from jax import lax
from jax.experimental import pallas as pl
from jax.experimental.pallas import tpu as pltpu
from jax.sharding import PartitionSpec as P

HD = 64
KSRC = 4
DISP = 2
GROUP = 4
LANES = GROUP * HD
LOG2E = 1.4426950408889634
F32 = jnp.float32
BF16 = jnp.bfloat16


def dot(a, b):
    return jnp.dot(a, b, preferred_element_type=F32)


def shift_columns(left, mid, right, width):
    count = mid.shape[0]
    col = lax.broadcasted_iota(jnp.int32, mid.shape, 0) % width
    return (
        mid
        + jnp.where(col == 0, 0.0, pltpu.roll(left, 1, 0))
        + jnp.where(col == width - 1, 0.0, pltpu.roll(right, count - 1, 0))
    )


def kernel(
    ids, valid, x, wc_hbm, wq_hbm, wk_hbm, wv_hbm, bias, gq, gk,
    feats, attended,
    ext, wc, wq, wk, wv, reach, q, keys, values, kdiag, vdiag, parts, acc, sums, mean,
    local_sem, send_sem, recv_sem,
):
    rows, width, chans = x.shape
    groups = chans // LANES
    frame, band = lax.axis_index("frame"), lax.axis_index("row")
    frames, bands = lax.axis_size("frame"), lax.axis_size("row")
    has_prev, has_next = frame > 0, frame < frames - 1
    has_above, has_below = band > 0, band < bands - 1
    to_above, to_below, to_next = {"row": band - 1}, {"row": band + 1}, {"frame": frame + 1}

    def fetch(i, src, dst):
        return pltpu.make_async_copy(src, dst, local_sem.at[i])

    def send(i, src, dst, device):
        return pltpu.make_async_remote_copy(
            src_ref=src,
            dst_ref=dst,
            send_sem=send_sem.at[i],
            recv_sem=recv_sem.at[i],
            device_id=device,
            device_id_type=pl.DeviceIdType.MESH,
        )

    barrier = pltpu.get_barrier_semaphore()
    met = 0
    for there, device in (
        (has_above, to_above),
        (has_below, to_below),
        (has_prev, {"frame": frame - 1}),
        (has_next, to_next),
    ):
        met = met + there.astype(jnp.int32)

        @pl.when(there)
        def _():
            pl.semaphore_signal(
                barrier, inc=1, device_id=device, device_id_type=pl.DeviceIdType.MESH
            )

    load_x = fetch(0, x, ext.at[pl.ds(1, rows)])
    load_x.start()
    middle = chans // 2
    halves = (pl.ds(0, middle), pl.ds(middle, middle))
    taps = [
        [
            fetch(1 + 3 * i + b, wc_hbm.at[:, b, :, half], wc.at[b, :, :, half])
            for b in range(3)
        ]
        for i, half in enumerate(halves)
    ]
    mats = [
        fetch(7 + i, src, dst)
        for i, (src, dst) in enumerate(
            ((wq_hbm, wq), (wk_hbm, wk), (wv_hbm, wv))
        )
    ]
    for copy in taps[0]:
        copy.start()

    kdiag[...] = jnp.zeros(kdiag.shape, BF16)
    vdiag[...] = jnp.zeros(vdiag.shape, BF16)
    row = lax.broadcasted_iota(jnp.int32, (LANES, LANES), 0) // HD
    col = lax.broadcasted_iota(jnp.int32, (LANES, LANES), 1) // HD
    mean[...] = jnp.where(row == col, 1.0 / HD, 0.0).astype(BF16)

    blank = jnp.zeros((width, chans), BF16)

    @pl.when(band == 0)
    def _():
        ext[0] = blank
        for i in range(DISP):
            reach[i] = blank

    @pl.when(band == bands - 1)
    def _():
        ext[rows + 1] = blank
        for i in range(DISP):
            reach[DISP + rows + i] = blank

    @pl.when(frame == 0)
    def _():
        for i in range(rows + 2 * DISP):
            reach[i] = blank

    halo_up = send(0, x.at[0], ext.at[rows + 1], to_above)
    halo_down = send(1, x.at[rows - 1], ext.at[0], to_below)

    edges = [(1, rows - 2), (0, rows - 1)]
    moves = []
    for r in range(rows):
        at = [2 + r]
        if r in edges[0]:
            at.append(2 + rows + 2 * DISP + edges[0].index(r))
        cuts = halves if r in edges[0] else (pl.ds(0, chans),)
        moves.append(
            [
                send(i, feats.at[r, :, cut], reach.at[DISP + r, :, cut], to_next)
                for i, cut in zip(at, cuts)
            ]
        )
    relays = {}
    for i in range(DISP):
        relays[i] = (
            send(2 + rows + i, reach.at[DISP + i], reach.at[DISP + rows + i], to_above),
            has_above,
            has_below,
            DISP + rows + i,
        )
        r = rows - DISP + i
        relays[r] = (
            send(2 + rows + DISP + i, reach.at[DISP + r], reach.at[i], to_below),
            has_below,
            has_above,
            i,
        )

    inner = [tuple(range(r, min(r + 2, rows - DISP))) for r in range(DISP, rows - DISP, 2)]

    def convolve(chunk, lanes):
        size = len(chunk) * width
        for b in range(3):
            window = jnp.concatenate(
                [jnp.concatenate([ext[r + a] for r in chunk], axis=0) for a in range(3)],
                axis=1,
            )
            kernel_b = wc[b, :, :, lanes]
            parts[b, 0:size, lanes] = dot(window, kernel_b.reshape(3 * chans, -1))
        total = shift_columns(*(parts[b, 0:size, lanes] for b in range(3)), width)
        total = (total + bias[:, lanes]).astype(BF16)
        for j, r in enumerate(chunk):
            feats[r, :, lanes] = total[j * width : (j + 1) * width]

    whole = pl.ds(0, chans)

    def forward(copies):
        @pl.when(has_next)
        def _():
            for copy in copies:
                copy.start()

    def normed(flat, weight, gain):
        proj = dot(flat, weight[...])
        square = (proj * proj).astype(BF16)
        square = jnp.concatenate(
            [dot(square[:, g * LANES : (g + 1) * LANES], mean[...]) for g in range(groups)],
            axis=1,
        )
        return (proj * lax.rsqrt(square + 1e-06) * gain).astype(BF16)

    half = lax.broadcasted_iota(jnp.int32, (width, 2 * HD), 1) // HD

    def diagonal(ref, slot, value):
        for g in range(groups):
            for h in range(GROUP):
                lane = g * LANES + h // 2 * 2 * HD
                tile = value[:, lane : lane + 2 * HD]
                lane = h // 2 * 2 * HD
                ref[slot, g, h * width : (h + 1) * width, lane : lane + 2 * HD] = jnp.where(
                    half == h % 2, tile, jnp.zeros_like(tile)
                )

    def attend(slot, first, last, counts):
        span = slice(first * width, last * width)
        probs = []
        for g in range(groups):
            lanes = slice(g * LANES, (g + 1) * LANES)
            expo = jnp.exp2(
                lax.dot_general(
                    q[span, lanes],
                    kdiag[slot, g],
                    (((1,), (1,)), ((), ())),
                    preferred_element_type=F32,
                )
            )
            if counts is None:
                sums[g, span] = expo
            else:
                expo = jnp.concatenate(
                    [
                        expo[i * width : (i + 1) * width] * count
                        for i, count in enumerate(counts)
                    ],
                    axis=0,
                )
                sums[g, span] = sums[g, span] + expo
            probs.append(expo.astype(BF16))
        mixed = [dot(probs[g], vdiag[slot, g]) for g in range(groups)]
        for g in range(groups):
            lanes = slice(g * LANES, (g + 1) * LANES)
            if counts is None:
                acc[span, lanes] = mixed[g]
            else:
                acc[span, lanes] = acc[span, lanes] + mixed[g]

    def project(first, last):
        span = slice(first * width, last * width)
        flat = feats[first:last].reshape((last - first) * width, chans)
        q[span] = normed(flat, wq, gq[...] * (LOG2E * HD**-0.5))
        keys[span] = normed(flat, wk, gk[...])
        values[span] = dot(flat, wv[...]).astype(BF16)

    load_x.wait()
    for b in range(3):
        taps[0][b].wait()
        taps[1][b].start()
    convolve(edges[0], halves[0])
    pl.semaphore_wait(barrier, met)
    forward([moves[r][0] for r in edges[0]])

    @pl.when(has_above)
    def _():
        halo_up.start()

    @pl.when(has_below)
    def _():
        halo_down.start()

    for copy in taps[1]:
        copy.wait()
    convolve(edges[0], halves[1])
    forward([moves[r][1] for r in edges[0]])
    for copy in mats:
        copy.start()
    for chunk in inner:
        convolve(chunk, whole)
    for copy in mats:
        copy.wait()
    project(1, rows - 1)

    @pl.when(has_above)
    def _():
        halo_down.wait_recv()

    @pl.when(has_below)
    def _():
        halo_up.wait_recv()

    convolve(edges[1], whole)
    forward([copy for chunk in edges[1:] + inner for r in chunk for copy in moves[r]])
    for r in edges[1]:
        project(r, r + 1)
    slots = kdiag.shape[0]
    for n in range(rows):
        span = slice(n * width, (n + 1) * width)
        diagonal(kdiag, n % slots, keys[span])
        diagonal(vdiag, n % slots, values[span])
        attend(n % slots, n, n + 1, None)

    live = has_prev.astype(jnp.int32)

    def named(n, place):
        count = 0
        for j in range(KSRC):
            here = ids[0, j, n] == band * rows + place - DISP
            count = count + (here & (j < valid[0, n])).astype(jnp.int32)
        return (count * live).astype(F32)

    def stages(places, k):
        flat = jnp.concatenate([reach[place] for place in places], axis=0)
        key = normed(flat, wk, gk[...])
        value = dot(flat, wv[...]).astype(BF16)
        for i, place in enumerate(places):
            slot = (k + i) % slots
            first, last = max(place - 2 * DISP, 0), min(place, rows - 1) + 1
            diagonal(kdiag, slot, key[i * width : (i + 1) * width])
            diagonal(vdiag, slot, value[i * width : (i + 1) * width])
            attend(slot, first, last, [named(n, place) for n in range(first, last)])

    side = lax.broadcasted_iota(jnp.int32, (width, 2 * HD), 1) // HD

    def finish(n):
        span = slice(n * width, (n + 1) * width)
        for g in range(groups):
            total = [
                jnp.sum(sums[g, span, h * width : (h + 1) * width], axis=1, keepdims=True)
                for h in range(GROUP)
            ]
            for h in range(0, GROUP, 2):
                lanes = slice(g * LANES + h * HD, g * LANES + (h + 2) * HD)
                inverse = 1.0 / jnp.where(side == 0, total[h], total[h + 1])
                attended[n, :, lanes] = (acc[span, lanes] * inverse).astype(BF16)

    steps = []
    late = []
    for r in [r for chunk in edges + inner for r in chunk]:
        step = [(moves[r], None, DISP + r, r)]
        if len(late) > 1:
            step.append(late.pop(0))
        steps.append(step)
        if r in relays:
            relay, _, arriving, place = relays[r]
            late.append(([relay], arriving, place, None))
    steps[-1:-1] = [[entry] for entry in late]

    left = [2 * DISP + 1] * rows
    k = 0
    for step in steps:
        for copies, arriving, _, r in step:

            @pl.when(has_prev if arriving is None else has_prev & arriving)
            def _():
                for copy in copies:
                    copy.wait_recv()

            if r in relays:
                relay, leaving, _, _ = relays[r]

                @pl.when(has_prev & leaving)
                def _():
                    relay.start()

        places = [place for _, _, place, _ in step]
        stages(places, k)
        k += len(places)
        for place in places:
            for n in range(max(place - 2 * DISP, 0), min(place, rows - 1) + 1):
                left[n] -= 1
                if left[n] == 0:
                    finish(n)

    @pl.when(has_above)
    def _():
        halo_up.wait_send()

    @pl.when(has_below)
    def _():
        halo_down.wait_send()

    @pl.when(has_next)
    def _():
        for copies in moves:
            for copy in copies:
                copy.wait_send()

    for relay, leaving, _, _ in relays.values():

        @pl.when(has_prev & leaving)
        def _():
            relay.wait_send()


def join(feats, attended, wo, out, stage, sem):
    rows, width, chans = feats.shape
    copies = []
    for r in range(rows):
        stage[r] = (feats[r].astype(F32) + dot(attended[r], wo[...])).astype(BF16)
        copies.append(pltpu.make_async_copy(stage.at[r], out.at[r], sem.at[r]))
        copies[r].start()
    for copy in copies:
        copy.wait()


VM = pl.BlockSpec(memory_space=pltpu.VMEM)
SM = pl.BlockSpec(memory_space=pltpu.SMEM)
ANY = pl.BlockSpec(memory_space=pltpu.HBM)


def shards(x, wc, bias, wq, wk, wv, wo, gq, gk, source_ids, valid_counts):
    x = x[0]
    rows, width, chans = x.shape
    groups = chans // LANES
    square = pltpu.VMEM((chans, chans), BF16)

    def stack(count):
        return pltpu.VMEM((count, width, chans), BF16)

    links = 4 + rows + 2 * DISP
    shape = jax.ShapeDtypeStruct((rows, width, chans), BF16)
    feats, attended = pl.pallas_call(
        kernel,
        out_shape=(pltpu.VMEM(shape.shape, BF16), pltpu.VMEM(shape.shape, BF16)),
        in_specs=[SM, SM] + [ANY] * 5 + [VM] * 3,
        out_specs=(VM, VM),
        scratch_shapes=[
            stack(rows + 2),
            pltpu.VMEM(wc.shape, BF16),
            square,
            square,
            square,
            stack(rows + 2 * DISP),
            pltpu.VMEM((rows * width, chans), BF16),
            pltpu.VMEM((rows * width, chans), BF16),
            pltpu.VMEM((rows * width, chans), BF16),
            pltpu.VMEM((4, groups, GROUP * width, LANES), BF16),
            pltpu.VMEM((4, groups, GROUP * width, LANES), BF16),
            pltpu.VMEM((3, 2 * width, chans), F32),
            pltpu.VMEM((rows * width, chans), F32),
            pltpu.VMEM((groups, rows * width, GROUP * width), F32),
            pltpu.VMEM((LANES, LANES), BF16),
            pltpu.SemaphoreType.DMA((10,)),
            pltpu.SemaphoreType.DMA((links,)),
            pltpu.SemaphoreType.DMA((links,)),
        ],
        compiler_params=pltpu.CompilerParams(
            vmem_limit_bytes=56 * 2**20, collective_id=0, has_side_effects=True
        ),
    )(jnp.swapaxes(source_ids, 1, 2), valid_counts, x, wc, wq, wk, wv, bias[None], gq[None], gk[None])
    out = pl.pallas_call(
        join,
        out_shape=shape,
        in_specs=[VM] * 3,
        out_specs=ANY,
        scratch_shapes=[
            pltpu.VMEM((rows, width, chans), BF16),
            pltpu.SemaphoreType.DMA((rows,)),
        ],
        compiler_params=pltpu.CompilerParams(vmem_limit_bytes=12 * 2**20),
    )(feats, attended, wo)
    return out[None]


def solution(mesh):
    return jax.shard_map(
        shards,
        mesh=mesh,
        in_specs=(P("frame", "row", None, None),)
        + (P(),) * 8
        + (P("frame", "row", None), P("frame", "row")),
        out_specs=P("frame", "row", None, None),
        check_vma=False,
    )
```

```python
import jax
import jax.numpy as jnp
from jax import lax
from jax.experimental import pallas as pl
from jax.experimental.pallas import tpu as pltpu
from jax.sharding import PartitionSpec as P

HD = 64
KSRC = 4
DISP = 2
GROUP = 4
LANES = GROUP * HD
LOG2E = 1.4426950408889634
F32 = jnp.float32
BF16 = jnp.bfloat16


def dot(a, b):
    return jnp.dot(a, b, preferred_element_type=F32)


def shift_columns(left, mid, right, width):
    count = mid.shape[0]
    col = lax.broadcasted_iota(jnp.int32, mid.shape, 0) % width
    return (
        mid
        + jnp.where(col == 0, 0.0, pltpu.roll(left, 1, 0))
        + jnp.where(col == width - 1, 0.0, pltpu.roll(right, count - 1, 0))
    )


def kernel(
    ids, valid, x, wc_hbm, wq_hbm, wk_hbm, wv_hbm, bias, gq, gk,
    feats, attended,
    ext, wc, wq, wk, wv, reach, q, keys, values, kdiag, vdiag, parts, acc, sums, mean,
    local_sem, send_sem, recv_sem,
):
    rows, width, chans = x.shape
    groups = chans // LANES
    frame, band = lax.axis_index("frame"), lax.axis_index("row")
    frames, bands = lax.axis_size("frame"), lax.axis_size("row")
    has_prev, has_next = frame > 0, frame < frames - 1
    has_above, has_below = band > 0, band < bands - 1
    to_above, to_below, to_next = {"row": band - 1}, {"row": band + 1}, {"frame": frame + 1}

    def fetch(i, src, dst):
        return pltpu.make_async_copy(src, dst, local_sem.at[i])

    def send(i, src, dst, device):
        return pltpu.make_async_remote_copy(
            src_ref=src,
            dst_ref=dst,
            send_sem=send_sem.at[i],
            recv_sem=recv_sem.at[i],
            device_id=device,
            device_id_type=pl.DeviceIdType.MESH,
        )

    barrier = pltpu.get_barrier_semaphore()
    met = 0
    for there, device in (
        (has_above, to_above),
        (has_below, to_below),
        (has_prev, {"frame": frame - 1}),
        (has_next, to_next),
    ):
        met = met + there.astype(jnp.int32)

        @pl.when(there)
        def _():
            pl.semaphore_signal(
                barrier, inc=1, device_id=device, device_id_type=pl.DeviceIdType.MESH
            )

    load_x = fetch(0, x, ext.at[pl.ds(1, rows)])
    load_x.start()
    middle = chans // 2
    halves = (pl.ds(0, middle), pl.ds(middle, middle))
    taps = [
        [
            fetch(1 + 3 * i + b, wc_hbm.at[:, b, :, half], wc.at[b, :, :, half])
            for b in range(3)
        ]
        for i, half in enumerate(halves)
    ]
    mats = [
        fetch(7 + i, src, dst)
        for i, (src, dst) in enumerate(
            ((wq_hbm, wq), (wk_hbm, wk), (wv_hbm, wv))
        )
    ]
    for copy in taps[0]:
        copy.start()

    kdiag[...] = jnp.zeros(kdiag.shape, BF16)
    vdiag[...] = jnp.zeros(vdiag.shape, BF16)
    row = lax.broadcasted_iota(jnp.int32, (LANES, LANES), 0) // HD
    col = lax.broadcasted_iota(jnp.int32, (LANES, LANES), 1) // HD
    mean[...] = jnp.where(row == col, 1.0 / HD, 0.0).astype(BF16)

    blank = jnp.zeros((width, chans), BF16)

    @pl.when(band == 0)
    def _():
        ext[0] = blank
        for i in range(DISP):
            reach[i] = blank

    @pl.when(band == bands - 1)
    def _():
        ext[rows + 1] = blank
        for i in range(DISP):
            reach[DISP + rows + i] = blank

    @pl.when(frame == 0)
    def _():
        for i in range(rows + 2 * DISP):
            reach[i] = blank

    halo_up = send(0, x.at[0], ext.at[rows + 1], to_above)
    halo_down = send(1, x.at[rows - 1], ext.at[0], to_below)

    edges = [(1, rows - 2), (0, rows - 1)]
    moves = []
    for r in range(rows):
        at = [2 + r]
        if r in edges[0]:
            at.append(2 + rows + 2 * DISP + edges[0].index(r))
        cuts = halves if r in edges[0] else (pl.ds(0, chans),)
        moves.append(
            [
                send(i, feats.at[r, :, cut], reach.at[DISP + r, :, cut], to_next)
                for i, cut in zip(at, cuts)
            ]
        )
    relays = {}
    for i in range(DISP):
        relays[i] = (
            send(2 + rows + i, reach.at[DISP + i], reach.at[DISP + rows + i], to_above),
            has_above,
            has_below,
            DISP + rows + i,
        )
        r = rows - DISP + i
        relays[r] = (
            send(2 + rows + DISP + i, reach.at[DISP + r], reach.at[i], to_below),
            has_below,
            has_above,
            i,
        )

    inner = [tuple(range(r, min(r + 2, rows - DISP))) for r in range(DISP, rows - DISP, 2)]

    def convolve(chunk, lanes, between=None):
        size = len(chunk) * width
        for b in range(3):
            if b == 1 and between is not None:
                between()
            window = jnp.concatenate(
                [jnp.concatenate([ext[r + a] for r in chunk], axis=0) for a in range(3)],
                axis=1,
            )
            kernel_b = wc[b, :, :, lanes]
            parts[b, 0:size, lanes] = dot(window, kernel_b.reshape(3 * chans, -1))
        total = shift_columns(*(parts[b, 0:size, lanes] for b in range(3)), width)
        total = (total + bias[:, lanes]).astype(BF16)
        for j, r in enumerate(chunk):
            feats[r, :, lanes] = total[j * width : (j + 1) * width]

    whole = pl.ds(0, chans)

    def forward(copies):
        @pl.when(has_next)
        def _():
            for copy in copies:
                copy.start()

    def normed(flat, weight, gain):
        proj = dot(flat, weight[...])
        square = (proj * proj).astype(BF16)
        square = jnp.concatenate(
            [dot(square[:, g * LANES : (g + 1) * LANES], mean[...]) for g in range(groups)],
            axis=1,
        )
        return (proj * lax.rsqrt(square + 1e-06) * gain).astype(BF16)

    half = lax.broadcasted_iota(jnp.int32, (width, 2 * HD), 1) // HD

    def diagonal(ref, slot, value):
        for g in range(groups):
            for h in range(GROUP):
                lane = g * LANES + h // 2 * 2 * HD
                tile = value[:, lane : lane + 2 * HD]
                lane = h // 2 * 2 * HD
                ref[slot, g, h * width : (h + 1) * width, lane : lane + 2 * HD] = jnp.where(
                    half == h % 2, tile, jnp.zeros_like(tile)
                )

    def attend(slot, first, last, counts):
        span = slice(first * width, last * width)
        probs = []
        for g in range(groups):
            lanes = slice(g * LANES, (g + 1) * LANES)
            expo = jnp.exp2(
                lax.dot_general(
                    q[span, lanes],
                    kdiag[slot, g],
                    (((1,), (1,)), ((), ())),
                    preferred_element_type=F32,
                )
            )
            if counts is None:
                sums[g, span] = expo
            else:
                expo = jnp.concatenate(
                    [
                        expo[i * width : (i + 1) * width] * count
                        for i, count in enumerate(counts)
                    ],
                    axis=0,
                )
                sums[g, span] = sums[g, span] + expo
            probs.append(expo.astype(BF16))
        mixed = [dot(probs[g], vdiag[slot, g]) for g in range(groups)]
        for g in range(groups):
            lanes = slice(g * LANES, (g + 1) * LANES)
            if counts is None:
                acc[span, lanes] = mixed[g]
            else:
                acc[span, lanes] = acc[span, lanes] + mixed[g]

    def project(first, last):
        span = slice(first * width, last * width)
        flat = feats[first:last].reshape((last - first) * width, chans)
        q[span] = normed(flat, wq, gq[...] * (LOG2E * HD**-0.5))
        keys[span] = normed(flat, wk, gk[...])
        values[span] = dot(flat, wv[...]).astype(BF16)

    load_x.wait()
    for b in range(3):
        taps[0][b].wait()
        taps[1][b].start()

    def greet():
        pl.semaphore_wait(barrier, met)

        @pl.when(has_above)
        def _():
            halo_up.start()

        @pl.when(has_below)
        def _():
            halo_down.start()

    convolve(edges[0], halves[0], greet)
    forward([moves[r][0] for r in edges[0]])

    for copy in taps[1]:
        copy.wait()
    convolve(edges[0], halves[1])
    forward([moves[r][1] for r in edges[0]])
    for copy in mats:
        copy.start()
    for chunk in inner:
        convolve(chunk, whole)
    for copy in mats:
        copy.wait()
    project(1, rows - 1)

    @pl.when(has_above)
    def _():
        halo_down.wait_recv()

    @pl.when(has_below)
    def _():
        halo_up.wait_recv()

    convolve(edges[1], whole)
    forward([copy for chunk in edges[1:] + inner for r in chunk for copy in moves[r]])
    for r in edges[1]:
        project(r, r + 1)
    slots = kdiag.shape[0]
    for n in range(rows):
        span = slice(n * width, (n + 1) * width)
        diagonal(kdiag, n % slots, keys[span])
        diagonal(vdiag, n % slots, values[span])
        attend(n % slots, n, n + 1, None)

    live = has_prev.astype(jnp.int32)

    def named(n, place):
        count = 0
        for j in range(KSRC):
            here = ids[0, j, n] == band * rows + place - DISP
            count = count + (here & (j < valid[0, n])).astype(jnp.int32)
        return (count * live).astype(F32)

    def stages(places, k):
        flat = jnp.concatenate([reach[place] for place in places], axis=0)
        key = normed(flat, wk, gk[...])
        value = dot(flat, wv[...]).astype(BF16)
        for i, place in enumerate(places):
            slot = (k + i) % slots
            first, last = max(place - 2 * DISP, 0), min(place, rows - 1) + 1
            diagonal(kdiag, slot, key[i * width : (i + 1) * width])
            diagonal(vdiag, slot, value[i * width : (i + 1) * width])
            attend(slot, first, last, [named(n, place) for n in range(first, last)])

    side = lax.broadcasted_iota(jnp.int32, (width, 2 * HD), 1) // HD

    def finish(n):
        span = slice(n * width, (n + 1) * width)
        for g in range(groups):
            total = [
                jnp.sum(sums[g, span, h * width : (h + 1) * width], axis=1, keepdims=True)
                for h in range(GROUP)
            ]
            for h in range(0, GROUP, 2):
                lanes = slice(g * LANES + h * HD, g * LANES + (h + 2) * HD)
                inverse = 1.0 / jnp.where(side == 0, total[h], total[h + 1])
                attended[n, :, lanes] = (acc[span, lanes] * inverse).astype(BF16)

    steps = []
    late = []
    for r in [r for chunk in edges + inner for r in chunk]:
        step = [(moves[r], None, DISP + r, r)]
        if len(late) > 1:
            step.append(late.pop(0))
        steps.append(step)
        if r in relays:
            relay, _, arriving, place = relays[r]
            late.append(([relay], arriving, place, None))
    steps[-1:-1] = [[entry] for entry in late]

    left = [2 * DISP + 1] * rows
    k = 0
    for step in steps:
        for copies, arriving, _, r in step:

            @pl.when(has_prev if arriving is None else has_prev & arriving)
            def _():
                for copy in copies:
                    copy.wait_recv()

            if r in relays:
                relay, leaving, _, _ = relays[r]

                @pl.when(has_prev & leaving)
                def _():
                    relay.start()

        places = [place for _, _, place, _ in step]
        stages(places, k)
        k += len(places)
        for place in places:
            for n in range(max(place - 2 * DISP, 0), min(place, rows - 1) + 1):
                left[n] -= 1
                if left[n] == 0:
                    finish(n)

    @pl.when(has_above)
    def _():
        halo_up.wait_send()

    @pl.when(has_below)
    def _():
        halo_down.wait_send()

    @pl.when(has_next)
    def _():
        for copies in moves:
            for copy in copies:
                copy.wait_send()

    for relay, leaving, _, _ in relays.values():

        @pl.when(has_prev & leaving)
        def _():
            relay.wait_send()


def join(feats, attended, wo, out, stage, sem):
    rows, width, chans = feats.shape
    copies = []
    for r in range(rows):
        stage[r] = (feats[r].astype(F32) + dot(attended[r], wo[...])).astype(BF16)
        copies.append(pltpu.make_async_copy(stage.at[r], out.at[r], sem.at[r]))
        copies[r].start()
    for copy in copies:
        copy.wait()


VM = pl.BlockSpec(memory_space=pltpu.VMEM)
SM = pl.BlockSpec(memory_space=pltpu.SMEM)
ANY = pl.BlockSpec(memory_space=pltpu.HBM)


def shards(x, wc, bias, wq, wk, wv, wo, gq, gk, source_ids, valid_counts):
    x = x[0]
    rows, width, chans = x.shape
    groups = chans // LANES
    square = pltpu.VMEM((chans, chans), BF16)

    def stack(count):
        return pltpu.VMEM((count, width, chans), BF16)

    links = 4 + rows + 2 * DISP
    shape = jax.ShapeDtypeStruct((rows, width, chans), BF16)
    feats, attended = pl.pallas_call(
        kernel,
        out_shape=(pltpu.VMEM(shape.shape, BF16), pltpu.VMEM(shape.shape, BF16)),
        in_specs=[SM, SM] + [ANY] * 5 + [VM] * 3,
        out_specs=(VM, VM),
        scratch_shapes=[
            stack(rows + 2),
            pltpu.VMEM(wc.shape, BF16),
            square,
            square,
            square,
            stack(rows + 2 * DISP),
            pltpu.VMEM((rows * width, chans), BF16),
            pltpu.VMEM((rows * width, chans), BF16),
            pltpu.VMEM((rows * width, chans), BF16),
            pltpu.VMEM((4, groups, GROUP * width, LANES), BF16),
            pltpu.VMEM((4, groups, GROUP * width, LANES), BF16),
            pltpu.VMEM((3, 2 * width, chans), F32),
            pltpu.VMEM((rows * width, chans), F32),
            pltpu.VMEM((groups, rows * width, GROUP * width), F32),
            pltpu.VMEM((LANES, LANES), BF16),
            pltpu.SemaphoreType.DMA((10,)),
            pltpu.SemaphoreType.DMA((links,)),
            pltpu.SemaphoreType.DMA((links,)),
        ],
        compiler_params=pltpu.CompilerParams(
            vmem_limit_bytes=56 * 2**20, collective_id=0, has_side_effects=True
        ),
    )(jnp.swapaxes(source_ids, 1, 2), valid_counts, x, wc, wq, wk, wv, bias[None], gq[None], gk[None])
    out = pl.pallas_call(
        join,
        out_shape=shape,
        in_specs=[VM] * 3,
        out_specs=ANY,
        scratch_shapes=[
            pltpu.VMEM((rows, width, chans), BF16),
            pltpu.SemaphoreType.DMA((rows,)),
        ],
        compiler_params=pltpu.CompilerParams(vmem_limit_bytes=12 * 2**20),
    )(feats, attended, wo)
    return out[None]


def solution(mesh):
    return jax.shard_map(
        shards,
        mesh=mesh,
        in_specs=(P("frame", "row", None, None),)
        + (P(),) * 8
        + (P("frame", "row", None), P("frame", "row")),
        out_specs=P("frame", "row", None, None),
        check_vma=False,
    )
```
